256 devices in a mesh: rep: 4 (over z_hi), fsdp: 64 (over y, z_lo, x, core).
Axes of the slice: x: 4, y: 4, z: 8 (z_hi: 4, z_lo: 2; z = z_hi * 2 + z_lo), core: 2. Of those that a mesh axis runs over, the one named last changes fastest.
Arguments:
- activations: bfloat16 [49152, 8192], P(('rep', 'fsdp')), may hold values from -6 to 6
- cotangent: bfloat16 [49152, 14336], P(('rep', 'fsdp')), may hold values from -0.109375 to 0.109375
- projector: bfloat16 [8192, 256], P('fsdp'), may hold values from -0.0625 to 0.0625
- moment1: float32 [256, 14336], P(None, 'fsdp'), may hold values from -4 to 4
- moment2: float32 [256, 14336], P(None, 'fsdp'), may hold values from 0.1 to 4
Outputs:
- moment1_new: float32 [256, 14336], P(None, 'fsdp')
- moment2_new: float32 [256, 14336], P(None, 'fsdp')
- update: bfloat16 [8192, 14336], P(None, 'fsdp')
The draws below stay inside these ranges and needn't reach their ends.
All inputs are finite; a program needn't handle non-finite values.
Results may differ from the reference program's by a relative error of at most 0.0051.
Values may be sent and summed in bfloat16 or wider, within the bound.
A program may use at most 128 MiB of HBM per device.

```python
import math
import jax
import jax.numpy as jnp
from jax import lax

D = 8192
FF = 14336
R = 256
STEP = 100
TOK_DEV = 192
TOKENS = 49152


def spiked(result, rng, source, target, shards_of, factor):
    owner, partner = [(jnp.arange(result.shape[dim]) // (result.shape[dim] // shards_of)).reshape([-1 if axis == dim else 1 for axis in range(result.ndim)]) for dim in (source, target)]
    chosen = jax.random.permutation(rng, shards_of)[partner]
    strong = (owner == chosen) | (owner == (partner + shards_of // 2) % shards_of)
    return jnp.where(strong, factor * result, result)


def block_scale(rng, shape, split, low, high):
    def one(dim, parts):
        heights = jax.random.uniform(jax.random.fold_in(jax.random.fold_in(rng, 6), dim), (parts,), jnp.float32, low / len(split), high / len(split))
        return jnp.repeat(jnp.exp(heights), shape[dim] // parts).reshape((-1,) + (1,) * (len(shape) - dim - 1))

    loudness = one(*split[0])
    for cut in split[1:]:
        loudness = loudness * one(*cut)
    return loudness


def scatter_about(own_key, dims, width, limit, cuts=(), dtype=jnp.bfloat16):
    drawn = width * jax.random.normal(own_key, dims, jnp.float32)
    if cuts:
        drawn = drawn * block_scale(own_key, dims, cuts, -0.22, 0.18)
    return jnp.clip(drawn, -limit, limit).astype(dtype)


def heavy_noise(own_key, dims, deviation, reach, pieces, heavy, kind=jnp.bfloat16):
    entries = deviation * jax.random.normal(own_key, dims, jnp.float32)
    if pieces:
        entries = entries * block_scale(own_key, dims, pieces, -0.22, 0.18)
    return jnp.clip(spiked(entries, jax.random.fold_in(own_key, 3), *heavy), -reach, reach).astype(kind)


def setup_inputs(seed: int = 0) -> dict:
    splits = jax.random.split(jax.random.key(seed), 6)
    return {
        "activations": scatter_about(splits[0], (TOKENS, D), 1.0, 6.0, ((0, 256),)),
        "cotangent": heavy_noise(splits[1], (TOKENS, FF), (TOKENS ** -0.5), 0.109375, ((0, 256),), (0, 1, 256, 6.0)),
        "projector": scatter_about(splits[2], (D, R), D ** -0.5, 0.0625, ((0, 64),)),
        "moment1": scatter_about(splits[3], (R, FF), 0.5, 4.0, ((1, 64),), jnp.float32),
        "moment2": jnp.clip(jnp.exp(math.log(4.0) - 3.6888794 * jax.random.uniform(splits[4], (R, FF), jnp.float32) ** block_scale(splits[4], (R, FF), ((1, 64),), -0.2, 0.2)), 0.1, 4.0),
    }


def reference(activations, cotangent, projector, moment1, moment2):
    blocks_count = TOKENS // TOK_DEV
    act_blocks = activations.reshape(blocks_count, TOK_DEV, D)
    cot_blocks = cotangent.reshape(blocks_count, TOK_DEV, FF)
    proj_wide = projector.astype(jnp.float32)

    def accumulate(running, pair):
        act_rows, cot_rows = pair
        low = jnp.dot(act_rows.astype(jnp.float32), proj_wide, precision=lax.Precision.HIGHEST)
        low = low.astype(jnp.bfloat16).astype(jnp.float32)
        grad_term = jnp.dot(low.T, cot_rows.astype(jnp.float32), precision=lax.Precision.HIGHEST)
        return (running + grad_term, None)
    grad, _ = lax.scan(accumulate, jnp.zeros((R, FF), jnp.float32), (act_blocks, cot_blocks))
    moment1_new = 0.9 * moment1 + 0.1 * grad
    moment2_new = 0.999 * moment2 + 0.001 * grad * grad
    first_fix = 1.0 - 0.9 ** STEP
    second_fix = 1.0 - 0.999 ** STEP
    direction = (moment1_new / first_fix / (jnp.sqrt(moment2_new / second_fix) + 1e-08)).astype(jnp.bfloat16)
    update = jnp.dot(projector, direction, preferred_element_type=jnp.float32).astype(jnp.bfloat16)
    return (moment1_new, moment2_new, update)
```

```python
import jax
import jax.numpy as jnp
from jax import lax
from jax.sharding import Mesh
from jax.sharding import PartitionSpec as P

STEP = 100

SUB = ("y", "zl", "x", "core")


def adam_moments(grad, moment1, moment2):
    return (0.9 * moment1 + 0.1 * grad, 0.999 * moment2 + 0.001 * grad * grad)


def gather_projector(projector, sizes):
    rows, width = projector.shape
    full = projector
    for name in ("y", "x", "zl", "core"):
        full = lax.all_gather(full, name, axis=0, tiled=False)
    full = jnp.transpose(full, (3, 1, 2, 0, 4, 5))
    return full.reshape(-1, width)


def body(activations, cotangent, projector, moment1, moment2):
    sizes = {n: lax.axis_size(n) for n in SUB}
    proj_full = gather_projector(projector, sizes)
    low = jnp.dot(activations, proj_full, preferred_element_type=jnp.float32).astype(jnp.bfloat16)
    terms = lax.dot_general(
        cotangent, low, (((0,), (0,)), ((), ())), preferred_element_type=jnp.float32
    )
    ff, rank = terms.shape
    cols = ff // (sizes["y"] * sizes["zl"] * sizes["x"] * sizes["core"])
    terms = terms.reshape(sizes["y"], sizes["zl"], sizes["x"], sizes["core"], cols, rank)
    terms = jnp.transpose(terms, (3, 2, 1, 0, 4, 5))
    for name in ("core", "x", "zl", "y"):
        terms = terms.reshape(sizes[name], -1, rank)
        terms = lax.psum_scatter(terms, name, scatter_dimension=0, tiled=True)
    group_grad = terms.reshape(cols, rank).T
    grad = lax.psum(group_grad, "rep")
    moment1_new, moment2_new = adam_moments(grad, moment1, moment2)
    first_fix = 1.0 - 0.9**STEP
    second_fix = 1.0 - 0.999**STEP
    direction = (moment1_new / first_fix / (jnp.sqrt(moment2_new / second_fix) + 1e-08)).astype(
        jnp.bfloat16
    )
    update = jnp.dot(proj_full, direction, preferred_element_type=jnp.float32)
    return (moment1_new, moment2_new, update.astype(jnp.bfloat16))


def solution(mesh):
    rep = mesh.shape["rep"]
    fsdp_devices = mesh.devices.reshape(rep, -1)
    n = fsdp_devices.shape[1]
    y, x, core = 4, 4, 2
    zl = n // (y * x * core)
    fine = Mesh(mesh.devices.reshape(rep, y, zl, x, core), ("rep",) + SUB)
    tok = ("rep",) + SUB
    return jax.shard_map(
        body,
        mesh=fine,
        in_specs=(
            P(tok, None),
            P(tok, None),
            P(SUB, None),
            P(None, SUB),
            P(None, SUB),
        ),
        out_specs=(P(None, SUB), P(None, SUB), P(None, SUB)),
        check_vma=False,
    )
```

```python
import jax
import jax.numpy as jnp
from jax import lax
from jax.sharding import Mesh
from jax.sharding import PartitionSpec as P

STEP = 100

SUB = ("y", "zl", "x", "core")


def adam_moments(grad, moment1, moment2):
    return (0.9 * moment1 + 0.1 * grad, 0.999 * moment2 + 0.001 * grad * grad)


def pair_swap(x, name):
    return lax.ppermute(x, name, [(0, 1), (1, 0)])


def gather_projector(projector, sizes):
    rows, width = projector.shape
    full = lax.all_gather(projector, "y", axis=0, tiled=False)
    full = lax.all_gather(full, "x", axis=0, tiled=False)
    other = pair_swap(full, "zl")
    first = lax.axis_index("zl") == 0
    full = jnp.stack([jnp.where(first, full, other), jnp.where(first, other, full)])
    full = lax.all_gather(full, "core", axis=0, tiled=False)
    full = jnp.transpose(full, (3, 1, 2, 0, 4, 5))
    return full.reshape(-1, width)


def all_sum_rep(x):
    size = lax.axis_size("rep")
    step = 1
    while step < size:
        x = x + lax.ppermute(x, "rep", [(i, i ^ step) for i in range(size)])
        step *= 2
    return x


def body(activations, cotangent, projector, moment1, moment2):
    sizes = {n: lax.axis_size(n) for n in SUB}
    proj_full = gather_projector(projector, sizes)
    low = jnp.dot(activations, proj_full, preferred_element_type=jnp.float32).astype(jnp.bfloat16)
    tok, ff = cotangent.shape
    cols = ff // (sizes["y"] * sizes["zl"] * sizes["x"] * sizes["core"])
    cot = cotangent.reshape(tok, sizes["y"], sizes["zl"], sizes["x"], sizes["core"], cols)
    cot = jnp.transpose(cot, (0, 4, 3, 2, 1, 5)).reshape(tok, ff)
    terms = lax.dot_general(cot, low, (((0,), (0,)), ((), ())), preferred_element_type=jnp.float32)
    rank = terms.shape[1]
    for name in ("core", "x"):
        terms = terms.reshape(sizes[name], -1, rank)
        terms = lax.psum_scatter(terms, name, scatter_dimension=0, tiled=True)
    terms = terms.reshape(sizes["zl"], -1, rank)
    z = lax.axis_index("zl")
    mine = lax.dynamic_index_in_dim(terms, z, 0, keepdims=False)
    theirs = lax.dynamic_index_in_dim(terms, 1 - z, 0, keepdims=False)
    terms = mine + pair_swap(theirs, "zl")
    terms = terms.reshape(sizes["y"], -1, rank)
    terms = lax.psum_scatter(terms, "y", scatter_dimension=0, tiled=True)
    group_grad = terms.reshape(cols, rank).T
    grad = all_sum_rep(group_grad)
    moment1_new, moment2_new = adam_moments(grad, moment1, moment2)
    first_fix = 1.0 - 0.9**STEP
    second_fix = 1.0 - 0.999**STEP
    direction = (moment1_new / first_fix / (jnp.sqrt(moment2_new / second_fix) + 1e-08)).astype(
        jnp.bfloat16
    )
    update = jnp.dot(proj_full, direction, preferred_element_type=jnp.float32)
    return (moment1_new, moment2_new, update.astype(jnp.bfloat16))


def solution(mesh):
    rep = mesh.shape["rep"]
    fsdp_devices = mesh.devices.reshape(rep, -1)
    n = fsdp_devices.shape[1]
    y, x, core = 4, 4, 2
    zl = n // (y * x * core)
    fine = Mesh(mesh.devices.reshape(rep, y, zl, x, core), ("rep",) + SUB)
    tok = ("rep",) + SUB
    return jax.shard_map(
        body,
        mesh=fine,
        in_specs=(
            P(tok, None),
            P(tok, None),
            P(SUB, None),
            P(None, SUB),
            P(None, SUB),
        ),
        out_specs=(P(None, SUB), P(None, SUB), P(None, SUB)),
        check_vma=False,
    )
```

```python
import jax
import jax.numpy as jnp
from jax import lax
from jax.sharding import Mesh
from jax.sharding import PartitionSpec as P

STEP = 100

SUB = ("y", "zl", "x", "core")
CHIPS = ("y", "zl", "x")


def adam_moments(grad, moment1, moment2):
    return (0.9 * moment1 + 0.1 * grad, 0.999 * moment2 + 0.001 * grad * grad)


def gather_projector(projector, sizes):
    rows, width = projector.shape
    full = lax.all_gather(projector, CHIPS, axis=0, tiled=False)
    full = lax.all_gather(full, "core", axis=0, tiled=False)
    full = jnp.transpose(full, (1, 0, 2, 3))
    return full.reshape(-1, width)


def all_sum_rep(x):
    size = lax.axis_size("rep")
    step = 1
    while step < size:
        x = x + lax.ppermute(x, "rep", [(i, i ^ step) for i in range(size)])
        step *= 2
    return x


def body(activations, cotangent, projector, moment1, moment2):
    sizes = {n: lax.axis_size(n) for n in SUB}
    chips = sizes["y"] * sizes["zl"] * sizes["x"]
    proj_full = gather_projector(projector, sizes)
    low = jnp.dot(activations, proj_full, preferred_element_type=jnp.float32).astype(jnp.bfloat16)
    terms = lax.dot_general(
        cotangent, low, (((0,), (0,)), ((), ())), preferred_element_type=jnp.float32
    )
    ff, rank = terms.shape
    cols = ff // (chips * sizes["core"])
    terms = terms.reshape(chips, sizes["core"], cols, rank)
    terms = jnp.transpose(terms, (1, 0, 2, 3)).reshape(sizes["core"], -1, rank)
    terms = lax.psum_scatter(terms, "core", scatter_dimension=0, tiled=True)
    terms = terms.reshape(chips, cols, rank)
    terms = lax.psum_scatter(terms, CHIPS, scatter_dimension=0, tiled=True)
    group_grad = terms.reshape(cols, rank).T
    grad = all_sum_rep(group_grad)
    moment1_new, moment2_new = adam_moments(grad, moment1, moment2)
    first_fix = 1.0 - 0.9**STEP
    second_fix = 1.0 - 0.999**STEP
    direction = (moment1_new / first_fix / (jnp.sqrt(moment2_new / second_fix) + 1e-08)).astype(
        jnp.bfloat16
    )
    update = jnp.dot(proj_full, direction, preferred_element_type=jnp.float32)
    return (moment1_new, moment2_new, update.astype(jnp.bfloat16))


def solution(mesh):
    rep = mesh.shape["rep"]
    fsdp_devices = mesh.devices.reshape(rep, -1)
    n = fsdp_devices.shape[1]
    y, x, core = 4, 4, 2
    zl = n // (y * x * core)
    fine = Mesh(mesh.devices.reshape(rep, y, zl, x, core), ("rep",) + SUB)
    tok = ("rep",) + SUB
    return jax.shard_map(
        body,
        mesh=fine,
        in_specs=(
            P(tok, None),
            P(tok, None),
            P(SUB, None),
            P(None, SUB),
            P(None, SUB),
        ),
        out_specs=(P(None, SUB), P(None, SUB), P(None, SUB)),
        check_vma=False,
    )
```

```python
import jax
import jax.numpy as jnp
from jax import lax
from jax.sharding import Mesh
from jax.sharding import PartitionSpec as P

STEP = 100

SUB = ("y", "zl", "x", "core")


def adam_moments(grad, moment1, moment2):
    return (0.9 * moment1 + 0.1 * grad, 0.999 * moment2 + 0.001 * grad * grad)


def pair_swap(x, name):
    return lax.ppermute(x, name, [(0, 1), (1, 0)])


def swap_stack(x, name):
    other = pair_swap(x, name)
    first = lax.axis_index(name) == 0
    return jnp.stack([jnp.where(first, x, other), jnp.where(first, other, x)])


def pair_sum_scatter(terms, name):
    i = lax.axis_index(name)
    mine = lax.dynamic_index_in_dim(terms, i, 0, keepdims=False)
    theirs = lax.dynamic_index_in_dim(terms, 1 - i, 0, keepdims=False)
    return mine + pair_swap(theirs, name)


def gather_projector(projector, sizes):
    rows, width = projector.shape
    full = lax.all_gather(projector, "y", axis=0, tiled=False)
    full = lax.all_gather(full, "x", axis=0, tiled=False)
    full = swap_stack(full, "zl")
    full = swap_stack(full, "core")
    full = jnp.transpose(full, (3, 1, 2, 0, 4, 5))
    return full.reshape(-1, width)


def all_sum_rep(x):
    size = lax.axis_size("rep")
    step = 1
    while step < size:
        x = x + lax.ppermute(x, "rep", [(i, i ^ step) for i in range(size)])
        step *= 2
    return x


def body(activations, cotangent, projector, moment1, moment2):
    sizes = {n: lax.axis_size(n) for n in SUB}
    proj_full = gather_projector(projector, sizes)
    low = jnp.dot(activations, proj_full, preferred_element_type=jnp.float32).astype(jnp.bfloat16)
    terms = lax.dot_general(
        cotangent, low, (((0,), (0,)), ((), ())), preferred_element_type=jnp.float32
    )
    ff, rank = terms.shape
    cols = ff // (sizes["y"] * sizes["zl"] * sizes["x"] * sizes["core"])
    terms = terms.reshape(sizes["y"], sizes["zl"], sizes["x"], sizes["core"], cols, rank)
    terms = jnp.transpose(terms, (3, 2, 1, 0, 4, 5)).reshape(sizes["core"], -1, rank)
    terms = pair_sum_scatter(terms, "core")
    terms = terms.reshape(sizes["x"], -1, rank)
    terms = lax.psum_scatter(terms, "x", scatter_dimension=0, tiled=True)
    terms = pair_sum_scatter(terms.reshape(sizes["zl"], -1, rank), "zl")
    terms = terms.reshape(sizes["y"], -1, rank)
    terms = lax.psum_scatter(terms, "y", scatter_dimension=0, tiled=True)
    group_grad = terms.reshape(cols, rank).T
    grad = all_sum_rep(group_grad)
    moment1_new, moment2_new = adam_moments(grad, moment1, moment2)
    first_fix = 1.0 - 0.9**STEP
    second_fix = 1.0 - 0.999**STEP
    direction = (moment1_new / first_fix / (jnp.sqrt(moment2_new / second_fix) + 1e-08)).astype(
        jnp.bfloat16
    )
    update = jnp.dot(proj_full, direction, preferred_element_type=jnp.float32)
    return (moment1_new, moment2_new, update.astype(jnp.bfloat16))


def solution(mesh):
    rep = mesh.shape["rep"]
    fsdp_devices = mesh.devices.reshape(rep, -1)
    n = fsdp_devices.shape[1]
    y, x, core = 4, 4, 2
    zl = n // (y * x * core)
    fine = Mesh(mesh.devices.reshape(rep, y, zl, x, core), ("rep",) + SUB)
    tok = ("rep",) + SUB
    return jax.shard_map(
        body,
        mesh=fine,
        in_specs=(
            P(tok, None),
            P(tok, None),
            P(SUB, None),
            P(None, SUB),
            P(None, SUB),
        ),
        out_specs=(P(None, SUB), P(None, SUB), P(None, SUB)),
        check_vma=False,
    )
```

```python
import jax
import jax.numpy as jnp
from jax import lax
from jax.sharding import Mesh
from jax.sharding import PartitionSpec as P

STEP = 100

SUB = ("y", "zl", "x", "core")


def adam_moments(grad, moment1, moment2):
    return (0.9 * moment1 + 0.1 * grad, 0.999 * moment2 + 0.001 * grad * grad)


def pair_swap(x, name):
    return lax.ppermute(x, name, [(0, 1), (1, 0)])


def swap_stack(x, name):
    other = pair_swap(x, name)
    first = lax.axis_index(name) == 0
    return jnp.stack([jnp.where(first, x, other), jnp.where(first, other, x)])


def pair_sum_scatter(terms, name):
    i = lax.axis_index(name)
    mine = lax.dynamic_index_in_dim(terms, i, 0, keepdims=False)
    theirs = lax.dynamic_index_in_dim(terms, 1 - i, 0, keepdims=False)
    return mine + pair_swap(theirs, name)


def gather_projector(projector, sizes):
    rows, width = projector.shape
    full = lax.all_gather(projector, "y", axis=0, tiled=False)
    full = lax.all_gather(full, "x", axis=0, tiled=False)
    full = swap_stack(full, "zl")
    full = swap_stack(full, "core")
    full = jnp.transpose(full, (3, 1, 2, 0, 4, 5))
    return full.reshape(-1, width)


def all_sum_rep(x):
    size = lax.axis_size("rep")
    step = 1
    while step < size:
        x = x + lax.ppermute(x, "rep", [(i, i ^ step) for i in range(size)])
        step *= 2
    return x


def reduce_terms(terms, sizes):
    ff, rank = terms.shape
    cols = ff // (sizes["y"] * sizes["zl"] * sizes["x"] * sizes["core"])
    terms = terms.reshape(sizes["y"], sizes["zl"], sizes["x"], sizes["core"], cols, rank)
    terms = jnp.transpose(terms, (3, 2, 1, 0, 4, 5)).reshape(sizes["core"], -1, rank)
    terms = pair_sum_scatter(terms, "core")
    terms = terms.reshape(sizes["x"], -1, rank)
    terms = lax.psum_scatter(terms, "x", scatter_dimension=0, tiled=True)
    terms = pair_sum_scatter(terms.reshape(sizes["zl"], -1, rank), "zl")
    terms = terms.reshape(sizes["y"], -1, rank)
    terms = lax.psum_scatter(terms, "y", scatter_dimension=0, tiled=True)
    return terms.reshape(cols, rank)


def body(activations, cotangent, projector, moment1, moment2):
    sizes = {n: lax.axis_size(n) for n in SUB}
    proj_full = gather_projector(projector, sizes)
    low = jnp.dot(activations, proj_full, preferred_element_type=jnp.float32).astype(jnp.bfloat16)
    rank = low.shape[1]
    chunks = 2
    width = rank // chunks
    parts = []
    for k in range(chunks):
        terms = lax.dot_general(
            cotangent,
            low[:, k * width : (k + 1) * width],
            (((0,), (0,)), ((), ())),
            preferred_element_type=jnp.float32,
        )
        parts.append(all_sum_rep(reduce_terms(terms, sizes)))
    grad = jnp.concatenate(parts, axis=1).T
    moment1_new, moment2_new = adam_moments(grad, moment1, moment2)
    first_fix = 1.0 - 0.9**STEP
    second_fix = 1.0 - 0.999**STEP
    direction = (moment1_new / first_fix / (jnp.sqrt(moment2_new / second_fix) + 1e-08)).astype(
        jnp.bfloat16
    )
    update = jnp.dot(proj_full, direction, preferred_element_type=jnp.float32)
    return (moment1_new, moment2_new, update.astype(jnp.bfloat16))


def solution(mesh):
    rep = mesh.shape["rep"]
    fsdp_devices = mesh.devices.reshape(rep, -1)
    n = fsdp_devices.shape[1]
    y, x, core = 4, 4, 2
    zl = n // (y * x * core)
    fine = Mesh(mesh.devices.reshape(rep, y, zl, x, core), ("rep",) + SUB)
    tok = ("rep",) + SUB
    return jax.shard_map(
        body,
        mesh=fine,
        in_specs=(
            P(tok, None),
            P(tok, None),
            P(SUB, None),
            P(None, SUB),
            P(None, SUB),
        ),
        out_specs=(P(None, SUB), P(None, SUB), P(None, SUB)),
        check_vma=False,
    )
```

```python
import jax
import jax.numpy as jnp
from jax import lax
from jax.sharding import Mesh
from jax.sharding import PartitionSpec as P

STEP = 100

SUB = ("y", "zl", "x", "core")


def adam_moments(grad, moment1, moment2):
    return (0.9 * moment1 + 0.1 * grad, 0.999 * moment2 + 0.001 * grad * grad)


def pair_swap(x, name, bit=1):
    size = lax.axis_size(name)
    return lax.ppermute(x, name, [(i, i ^ bit) for i in range(size)])


def swap_stack(x, name, bit=1):
    other = pair_swap(x, name, bit)
    first = (lax.axis_index(name) // bit) % 2 == 0
    return jnp.stack([jnp.where(first, x, other), jnp.where(first, other, x)])


def pair_sum_scatter(terms, name, bit=1):
    i = (lax.axis_index(name) // bit) % 2
    mine = lax.dynamic_index_in_dim(terms, i, 0, keepdims=False)
    theirs = lax.dynamic_index_in_dim(terms, 1 - i, 0, keepdims=False)
    return mine + pair_swap(theirs, name, bit)


def gather_projector(projector, sizes):
    rows, width = projector.shape
    full = swap_stack(swap_stack(projector, "y", 1), "y", 2)
    full = swap_stack(swap_stack(full, "x", 1), "x", 2)
    full = swap_stack(full, "zl")
    full = swap_stack(full, "core")
    full = full.reshape(sizes["core"], sizes["zl"], sizes["x"], sizes["y"], rows, width)
    full = jnp.transpose(full, (3, 1, 2, 0, 4, 5))
    return full.reshape(-1, width)


def all_sum_rep(x):
    size = lax.axis_size("rep")
    step = 1
    while step < size:
        x = x + lax.ppermute(x, "rep", [(i, i ^ step) for i in range(size)])
        step *= 2
    return x


def reduce_terms(terms, sizes):
    ff, rank = terms.shape
    cols = ff // (sizes["y"] * sizes["zl"] * sizes["x"] * sizes["core"])
    terms = terms.reshape(sizes["y"], sizes["zl"], sizes["x"], sizes["core"], cols, rank)
    terms = jnp.transpose(terms, (3, 2, 1, 0, 4, 5)).reshape(sizes["core"], -1, rank)
    terms = pair_sum_scatter(terms, "core")
    terms = terms.reshape(sizes["x"], -1, rank)
    terms = lax.psum_scatter(terms, "x", scatter_dimension=0, tiled=True)
    terms = pair_sum_scatter(terms.reshape(sizes["zl"], -1, rank), "zl")
    terms = pair_sum_scatter(terms.reshape(2, -1, rank), "y", 2)
    terms = pair_sum_scatter(terms.reshape(2, -1, rank), "y", 1)
    return terms.reshape(cols, rank)


def body(activations, cotangent, projector, moment1, moment2):
    sizes = {n: lax.axis_size(n) for n in SUB}
    proj_full = gather_projector(projector, sizes)
    low = jnp.dot(activations, proj_full, preferred_element_type=jnp.float32).astype(jnp.bfloat16)
    rank = low.shape[1]
    chunks = 2
    width = rank // chunks
    parts = []
    for k in range(chunks):
        terms = lax.dot_general(
            cotangent,
            low[:, k * width : (k + 1) * width],
            (((0,), (0,)), ((), ())),
            preferred_element_type=jnp.float32,
        )
        parts.append(all_sum_rep(reduce_terms(terms, sizes)))
    grad = jnp.concatenate(parts, axis=1).T
    moment1_new, moment2_new = adam_moments(grad, moment1, moment2)
    first_fix = 1.0 - 0.9**STEP
    second_fix = 1.0 - 0.999**STEP
    direction = (moment1_new / first_fix / (jnp.sqrt(moment2_new / second_fix) + 1e-08)).astype(
        jnp.bfloat16
    )
    update = jnp.dot(proj_full, direction, preferred_element_type=jnp.float32)
    return (moment1_new, moment2_new, update.astype(jnp.bfloat16))


def solution(mesh):
    rep = mesh.shape["rep"]
    fsdp_devices = mesh.devices.reshape(rep, -1)
    n = fsdp_devices.shape[1]
    y, x, core = 4, 4, 2
    zl = n // (y * x * core)
    fine = Mesh(mesh.devices.reshape(rep, y, zl, x, core), ("rep",) + SUB)
    tok = ("rep",) + SUB
    return jax.shard_map(
        body,
        mesh=fine,
        in_specs=(
            P(tok, None),
            P(tok, None),
            P(SUB, None),
            P(None, SUB),
            P(None, SUB),
        ),
        out_specs=(P(None, SUB), P(None, SUB), P(None, SUB)),
        check_vma=False,
    )
```

```python
import jax
import jax.numpy as jnp
from jax import lax
from jax.sharding import Mesh
from jax.sharding import PartitionSpec as P

STEP = 100

SUB = ("y", "zl", "x", "core")


def adam_moments(grad, moment1, moment2):
    return (0.9 * moment1 + 0.1 * grad, 0.999 * moment2 + 0.001 * grad * grad)


def pair_swap(x, name, bit=1):
    size = lax.axis_size(name)
    return lax.ppermute(x, name, [(i, i ^ bit) for i in range(size)])


def swap_stack(x, name, bit=1):
    other = pair_swap(x, name, bit)
    first = (lax.axis_index(name) // bit) % 2 == 0
    return jnp.stack([jnp.where(first, x, other), jnp.where(first, other, x)])


def pair_sum_scatter(terms, name, bit=1):
    i = (lax.axis_index(name) // bit) % 2
    mine = lax.dynamic_index_in_dim(terms, i, 0, keepdims=False)
    theirs = lax.dynamic_index_in_dim(terms, 1 - i, 0, keepdims=False)
    return mine + pair_swap(theirs, name, bit)


def gather_projector(projector, sizes):
    rows, width = projector.shape
    full = swap_stack(swap_stack(projector, "y", 1), "y", 2)
    full = swap_stack(swap_stack(full, "x", 1), "x", 2)
    full = swap_stack(full, "zl")
    full = swap_stack(full, "core")
    full = full.reshape(sizes["core"], sizes["zl"], sizes["x"], sizes["y"], rows, width)
    full = jnp.transpose(full, (3, 1, 2, 0, 4, 5))
    return full.reshape(-1, width)


def all_sum_rep(x):
    size = lax.axis_size("rep")
    step = 1
    while step < size:
        x = x + lax.ppermute(x, "rep", [(i, i ^ step) for i in range(size)])
        step *= 2
    return x


def reduce_terms(terms, sizes, pieces=2):
    ff, rank = terms.shape
    cols = ff // (sizes["y"] * sizes["zl"] * sizes["x"] * sizes["core"])
    terms = terms.reshape(sizes["y"], sizes["zl"], sizes["x"], sizes["core"], cols, rank)
    terms = jnp.transpose(terms, (3, 2, 1, 0, 4, 5))
    step = cols // pieces
    out = []
    for p in range(pieces):
        part = terms[:, :, :, :, p * step : (p + 1) * step, :].reshape(sizes["core"], -1, rank)
        part = pair_sum_scatter(part, "core")
        part = part.reshape(sizes["x"], -1, rank)
        part = lax.psum_scatter(part, "x", scatter_dimension=0, tiled=True)
        part = pair_sum_scatter(part.reshape(sizes["zl"], -1, rank), "zl")
        part = pair_sum_scatter(part.reshape(2, -1, rank), "y", 2)
        part = pair_sum_scatter(part.reshape(2, -1, rank), "y", 1)
        out.append(part.reshape(step, rank))
    return jnp.concatenate(out, axis=0)


def body(activations, cotangent, projector, moment1, moment2):
    sizes = {n: lax.axis_size(n) for n in SUB}
    proj_full = gather_projector(projector, sizes)
    low = jnp.dot(activations, proj_full, preferred_element_type=jnp.float32).astype(jnp.bfloat16)
    rank = low.shape[1]
    chunks = 2
    width = rank // chunks
    parts = []
    for k in range(chunks):
        terms = lax.dot_general(
            cotangent,
            low[:, k * width : (k + 1) * width],
            (((0,), (0,)), ((), ())),
            preferred_element_type=jnp.float32,
        )
        parts.append(all_sum_rep(reduce_terms(terms, sizes)))
    grad = jnp.concatenate(parts, axis=1).T
    moment1_new, moment2_new = adam_moments(grad, moment1, moment2)
    first_fix = 1.0 - 0.9**STEP
    second_fix = 1.0 - 0.999**STEP
    direction = (moment1_new / first_fix / (jnp.sqrt(moment2_new / second_fix) + 1e-08)).astype(
        jnp.bfloat16
    )
    update = jnp.dot(proj_full, direction, preferred_element_type=jnp.float32)
    return (moment1_new, moment2_new, update.astype(jnp.bfloat16))


def solution(mesh):
    rep = mesh.shape["rep"]
    fsdp_devices = mesh.devices.reshape(rep, -1)
    n = fsdp_devices.shape[1]
    y, x, core = 4, 4, 2
    zl = n // (y * x * core)
    fine = Mesh(mesh.devices.reshape(rep, y, zl, x, core), ("rep",) + SUB)
    tok = ("rep",) + SUB
    return jax.shard_map(
        body,
        mesh=fine,
        in_specs=(
            P(tok, None),
            P(tok, None),
            P(SUB, None),
            P(None, SUB),
            P(None, SUB),
        ),
        out_specs=(P(None, SUB), P(None, SUB), P(None, SUB)),
        check_vma=False,
    )
```

```python
import jax
import jax.numpy as jnp
from jax import lax
from jax.sharding import Mesh
from jax.sharding import PartitionSpec as P

STEP = 100

SUB = ("y", "zl", "x", "core")


def adam_moments(grad, moment1, moment2):
    return (0.9 * moment1 + 0.1 * grad, 0.999 * moment2 + 0.001 * grad * grad)


def pair_swap(x, name, bit=1):
    size = lax.axis_size(name)
    return lax.ppermute(x, name, [(i, i ^ bit) for i in range(size)])


def swap_stack(x, name, bit=1):
    other = pair_swap(x, name, bit)
    first = (lax.axis_index(name) // bit) % 2 == 0
    return jnp.stack([jnp.where(first, x, other), jnp.where(first, other, x)])


def pair_sum_scatter(terms, name, bit=1):
    i = (lax.axis_index(name) // bit) % 2
    mine = lax.dynamic_index_in_dim(terms, i, 0, keepdims=False)
    theirs = lax.dynamic_index_in_dim(terms, 1 - i, 0, keepdims=False)
    return mine + pair_swap(theirs, name, bit)


def gather_projector(projector, sizes):
    rows, width = projector.shape
    full = swap_stack(swap_stack(projector, "y", 2), "y", 1)
    full = swap_stack(swap_stack(full, "x", 2), "x", 1)
    full = swap_stack(full, "zl")
    full = swap_stack(full, "core")
    full = jnp.transpose(full, (5, 4, 1, 3, 2, 0, 6, 7))
    return full.reshape(-1, width)


def all_sum_rep(x):
    size = lax.axis_size("rep")
    step = 1
    while step < size:
        x = x + lax.ppermute(x, "rep", [(i, i ^ step) for i in range(size)])
        step *= 2
    return x


def reduce_terms(terms, sizes):
    ff, rank = terms.shape
    cols = ff // (sizes["y"] * sizes["zl"] * sizes["x"] * sizes["core"])
    terms = terms.reshape(2, 2, sizes["zl"], sizes["x"], sizes["core"], cols, rank)
    terms = jnp.transpose(terms, (4, 3, 2, 1, 0, 5, 6)).reshape(sizes["core"], -1, rank)
    terms = pair_sum_scatter(terms, "core")
    terms = terms.reshape(sizes["x"], -1, rank)
    terms = lax.psum_scatter(terms, "x", scatter_dimension=0, tiled=True)
    terms = pair_sum_scatter(terms.reshape(sizes["zl"], -1, rank), "zl")
    terms = pair_sum_scatter(terms.reshape(2, -1, rank), "y", 1)
    terms = pair_sum_scatter(terms.reshape(2, -1, rank), "y", 2)
    return terms.reshape(cols, rank)


def body(activations, cotangent, projector, moment1, moment2):
    sizes = {n: lax.axis_size(n) for n in SUB}
    proj_full = gather_projector(projector, sizes)
    low = jnp.dot(activations, proj_full, preferred_element_type=jnp.float32).astype(jnp.bfloat16)
    rank = low.shape[1]
    chunks = 2
    width = rank // chunks
    parts = []
    for k in range(chunks):
        terms = lax.dot_general(
            cotangent,
            low[:, k * width : (k + 1) * width],
            (((0,), (0,)), ((), ())),
            preferred_element_type=jnp.float32,
        )
        parts.append(all_sum_rep(reduce_terms(terms, sizes)))
    grad = jnp.concatenate(parts, axis=1).T
    moment1_new, moment2_new = adam_moments(grad, moment1, moment2)
    first_fix = 1.0 - 0.9**STEP
    second_fix = 1.0 - 0.999**STEP
    direction = (moment1_new / first_fix / (jnp.sqrt(moment2_new / second_fix) + 1e-08)).astype(
        jnp.bfloat16
    )
    update = jnp.dot(proj_full, direction, preferred_element_type=jnp.float32)
    return (moment1_new, moment2_new, update.astype(jnp.bfloat16))


def solution(mesh):
    rep = mesh.shape["rep"]
    fsdp_devices = mesh.devices.reshape(rep, -1)
    n = fsdp_devices.shape[1]
    y, x, core = 4, 4, 2
    zl = n // (y * x * core)
    fine = Mesh(mesh.devices.reshape(rep, y, zl, x, core), ("rep",) + SUB)
    tok = ("rep",) + SUB
    return jax.shard_map(
        body,
        mesh=fine,
        in_specs=(
            P(tok, None),
            P(tok, None),
            P(SUB, None),
            P(None, SUB),
            P(None, SUB),
        ),
        out_specs=(P(None, SUB), P(None, SUB), P(None, SUB)),
        check_vma=False,
    )
```

```python
import jax
import jax.numpy as jnp
from jax import lax
from jax.sharding import Mesh
from jax.sharding import PartitionSpec as P

STEP = 100

SUB = ("y", "zl", "x", "core")


def adam_moments(grad, moment1, moment2):
    return (0.9 * moment1 + 0.1 * grad, 0.999 * moment2 + 0.001 * grad * grad)


def pair_swap(x, name, bit=1):
    size = lax.axis_size(name)
    return lax.ppermute(x, name, [(i, i ^ bit) for i in range(size)])


def swap_stack(x, name, bit=1):
    other = pair_swap(x, name, bit)
    first = (lax.axis_index(name) // bit) % 2 == 0
    return jnp.stack([jnp.where(first, x, other), jnp.where(first, other, x)])


def pair_sum_scatter(terms, name, bit=1):
    i = (lax.axis_index(name) // bit) % 2
    mine = lax.dynamic_index_in_dim(terms, i, 0, keepdims=False)
    theirs = lax.dynamic_index_in_dim(terms, 1 - i, 0, keepdims=False)
    return mine + pair_swap(theirs, name, bit)


def gather_projector(projector, sizes):
    rows, width = projector.shape
    full = swap_stack(swap_stack(projector, "y", 2), "y", 1)
    full = swap_stack(swap_stack(full, "x", 2), "x", 1)
    full = swap_stack(full, "zl")
    full = swap_stack(full, "core")
    full = jnp.transpose(full, (5, 4, 1, 3, 2, 0, 6, 7))
    return full.reshape(-1, width)


def all_sum_rep(x):
    size = lax.axis_size("rep")
    step = 1
    while step < size:
        x = x + lax.ppermute(x, "rep", [(i, i ^ step) for i in range(size)])
        step *= 2
    return x


def reduce_terms(terms, sizes):
    ff, rank = terms.shape
    cols = ff // (sizes["y"] * sizes["zl"] * sizes["x"] * sizes["core"])
    terms = terms.reshape(2, 2, sizes["zl"], sizes["x"], sizes["core"], cols, rank)
    c = lax.axis_index("core")
    mine = lax.dynamic_index_in_dim(terms, c, 4, keepdims=False)
    theirs = lax.dynamic_index_in_dim(terms, 1 - c, 4, keepdims=False)
    terms = mine + pair_swap(theirs, "core")
    terms = jnp.transpose(terms, (3, 2, 1, 0, 4, 5)).reshape(sizes["x"], -1, rank)
    terms = lax.psum_scatter(terms, "x", scatter_dimension=0, tiled=True)
    terms = pair_sum_scatter(terms.reshape(sizes["zl"], -1, rank), "zl")
    terms = pair_sum_scatter(terms.reshape(2, -1, rank), "y", 1)
    terms = pair_sum_scatter(terms.reshape(2, -1, rank), "y", 2)
    return terms.reshape(cols, rank)


def body(activations, cotangent, projector, moment1, moment2):
    sizes = {n: lax.axis_size(n) for n in SUB}
    proj_full = gather_projector(projector, sizes)
    low = jnp.dot(activations, proj_full, preferred_element_type=jnp.float32).astype(jnp.bfloat16)
    rank = low.shape[1]
    chunks = 2
    width = rank // chunks
    parts = []
    for k in range(chunks):
        terms = lax.dot_general(
            cotangent,
            low[:, k * width : (k + 1) * width],
            (((0,), (0,)), ((), ())),
            preferred_element_type=jnp.float32,
        )
        parts.append(all_sum_rep(reduce_terms(terms, sizes)))
    grad = jnp.concatenate(parts, axis=1).T
    moment1_new, moment2_new = adam_moments(grad, moment1, moment2)
    first_fix = 1.0 - 0.9**STEP
    second_fix = 1.0 - 0.999**STEP
    direction = (moment1_new / first_fix / (jnp.sqrt(moment2_new / second_fix) + 1e-08)).astype(
        jnp.bfloat16
    )
    update = jnp.dot(proj_full, direction, preferred_element_type=jnp.float32)
    return (moment1_new, moment2_new, update.astype(jnp.bfloat16))


def solution(mesh):
    rep = mesh.shape["rep"]
    fsdp_devices = mesh.devices.reshape(rep, -1)
    n = fsdp_devices.shape[1]
    y, x, core = 4, 4, 2
    zl = n // (y * x * core)
    fine = Mesh(mesh.devices.reshape(rep, y, zl, x, core), ("rep",) + SUB)
    tok = ("rep",) + SUB
    return jax.shard_map(
        body,
        mesh=fine,
        in_specs=(
            P(tok, None),
            P(tok, None),
            P(SUB, None),
            P(None, SUB),
            P(None, SUB),
        ),
        out_specs=(P(None, SUB), P(None, SUB), P(None, SUB)),
        check_vma=False,
    )
```
